32 devices in a mesh: news: 2 (over x), entity: 16 (over z, y, core).
Axes of the slice: x: 2, y: 2, z: 4, core: 2. Of those that a mesh axis runs over, the one named last changes fastest.
Arguments:
- companies: bfloat16 [16384, 512], P('entity'), may hold values from -200 to 200
- queries: bfloat16 [256, 512], P(('news', 'entity')), may hold values from -2600 to 2600
Outputs:
- pooled: float32 [256, 512], P(('news', 'entity'))
The draws below stay inside these ranges and needn't reach their ends.
All inputs are finite; a program needn't handle non-finite values.
Results may differ from the reference program's by a relative error of at most 0.0076.
Values may be sent and summed in bfloat16 or wider, within the bound.
A program may use at most 64 MiB of HBM per device.

```python
import math
import jax
import jax.numpy as jnp
from jax import lax

D = 512
R_DEV = 1024
ITERS = 3
ROWS = 16384
QB = 128
NQ = 256
N_NEWS = 2


def slab_parts(key):
    column_order = jax.random.permutation(jax.random.fold_in(key, 108), D).astype(jnp.int32)
    spread = (column_order.astype(jnp.float32) + jax.random.uniform(jax.random.fold_in(key, 101), (D,), jnp.float32)) / D
    columns = jnp.exp(spread * math.log(10.0))
    low_half = (column_order < D // 2).astype(jnp.float32)
    group_count = D // 16
    group_index = jnp.minimum(column_order // 8, group_count - 1)
    group_factors = jnp.clip(jax.random.normal(jax.random.fold_in(key, 109), (ROWS, group_count), jnp.float32), -3.0, 3.0)
    group_part = jnp.take(group_factors, group_index, axis=1)
    block_count = ROWS // R_DEV
    loadings = jnp.clip(jax.random.normal(jax.random.fold_in(key, 110), (block_count, D), jnp.float32), -2.0, 2.0)
    sector = jnp.clip(jax.random.normal(jax.random.fold_in(key, 111), (ROWS,), jnp.float32), -3.0, 3.0)
    block_part = sector[:, None] * jnp.repeat(loadings, R_DEV, axis=0)
    structure = low_half[None, :] * (1.2 * group_part + 0.8 * block_part)
    row_scales = 0.5 * jnp.exp(jax.random.uniform(jax.random.fold_in(key, 102), (ROWS,), jnp.float32) * math.log(10.0))
    noise = jnp.clip(jax.random.normal(jax.random.fold_in(key, 103), (ROWS, D), jnp.float32), -4.0, 4.0)
    slab_values = (noise + structure) * columns[None, :] * row_scales[:, None]
    return (slab_values, columns)


def draw_companies(key, part):
    slab_values, columns = slab_parts(key)
    return slab_values.astype(jnp.bfloat16)


def draw_queries(key, part):
    slab_values, columns = slab_parts(key)
    query_scales = 0.5 * jnp.exp(jax.random.uniform(jax.random.fold_in(key, 107), (NQ,), jnp.float32) * math.log(4.0))
    noise = jnp.clip(jax.random.normal(jax.random.fold_in(key, 106), (NQ, D), jnp.float32), -4.0, 4.0)
    query_values = noise * columns[None, :] * query_scales[:, None]
    return query_values.astype(jnp.bfloat16)


def setup_inputs(seed: int = 0) -> dict:
    seeds = jax.random.split(jax.random.key(seed), 3)
    return {
        "companies": draw_companies(jax.random.fold_in(seeds[2], 71), 0),
        "queries": draw_queries(jax.random.fold_in(seeds[2], 71), 0),
    }


RIDGE = 0.05
EPSILON = 1e-06

def product(first_mat, second_mat):
    return jnp.dot(first_mat, second_mat, precision=lax.Precision.HIGHEST, preferred_element_type=jnp.float32)

def inverse_root(gram_full):
    identity = jnp.eye(D, dtype=jnp.float32)
    frob_norm = jnp.sqrt(jnp.sum(gram_full * gram_full) + EPSILON)
    y_iter = gram_full / frob_norm
    z_iter = identity
    for sweep_idx in range(ITERS):
        t_iter = 0.5 * (3.0 * identity - product(z_iter, y_iter))
        y_iter = product(y_iter, t_iter)
        z_iter = product(z_iter, t_iter)
    return (z_iter / jnp.sqrt(frob_norm)).astype(jnp.bfloat16)

def reference(companies, queries):
    gram_full = jnp.dot(companies.T, companies, preferred_element_type=jnp.float32) / ROWS
    gram_full = gram_full + RIDGE * jnp.eye(D, dtype=jnp.float32)
    whitener = inverse_root(gram_full)
    white_slab = jnp.dot(companies, whitener, preferred_element_type=jnp.float32).astype(jnp.bfloat16)
    white_query = jnp.dot(queries, whitener, preferred_element_type=jnp.float32).astype(jnp.bfloat16)
    score_scale = D ** (-0.5)

    def pool_block(query_block):
        scores = jnp.dot(query_block, white_slab.T, preferred_element_type=jnp.float32) * score_scale
        row_top = lax.optimization_barrier(jnp.max(scores, axis=1, keepdims=True))
        weights = jnp.exp(scores - row_top)
        denom = lax.optimization_barrier(jnp.sum(weights, axis=1))
        summed = jnp.dot(weights.astype(jnp.bfloat16), white_slab, preferred_element_type=jnp.float32)
        return summed / denom[:, None]
    pooled = lax.map(pool_block, white_query.reshape(N_NEWS, QB, D))
    return pooled.reshape(NQ, D)
```

```python
import functools

import jax
import jax.numpy as jnp
from jax import lax
from jax.experimental import pallas as pl
from jax.experimental.pallas import tpu as pltpu
from jax.sharding import PartitionSpec as P

RIDGE = 0.05
EPSILON = 1e-06
MESH = pl.DeviceIdType.MESH
LANES = 128
TILE = 16
F32 = jnp.float32
BF16 = jnp.bfloat16


def split(mat):
    high = mat.astype(BF16)
    return high, (mat - high.astype(F32)).astype(BF16)


def dot(first_mat, second_mat):
    return jnp.dot(first_mat, second_mat, preferred_element_type=F32)


def product(first_pair, second_pair):
    first_high, first_low = first_pair
    second_high, second_low = second_pair
    return (
        dot(first_low, second_high) + dot(first_high, second_low) + dot(first_high, second_high)
    )


def send_all(n_entity, make_copy):
    me = lax.axis_index("entity")
    for hop in range(1, n_entity):
        make_copy(hop, lax.rem(me + hop, n_entity)).start()


def wait_bytes(ref, sem):
    pltpu.make_async_copy(ref, ref, sem).wait()


def kernel(
    n_entity,
    comp_hbm,
    query_ref,
    out_ref,
    comp,
    query_all,
    query_f32,
    gram_send,
    gram_recv,
    gram_all,
    gram,
    sums,
    sums_send,
    sums_recv,
    stats,
    stats_recv,
    load_sem,
    send_sem,
    recv_sem,
):
    rows, width = comp.shape
    count = query_ref.shape[0]
    total_rows = rows * n_entity
    n_blocks = width // LANES
    per_piece = gram_send.shape[1]
    me = lax.axis_index("entity")

    load = pltpu.make_async_copy(comp_hbm, comp, load_sem)
    load.start()
    barrier = pltpu.get_barrier_semaphore()
    for hop in range(1, n_entity):
        pl.semaphore_signal(
            barrier,
            inc=1,
            device_id={"entity": lax.rem(me + hop, n_entity)},
            device_id_type=MESH,
        )
    query_all[me] = query_ref[...]
    load.wait()

    blocks = [(i, j) for i in range(n_blocks) for j in range(i, n_blocks)]
    per_block = LANES // TILE
    partial = {}
    for i in range(n_blocks):
        row_part = lax.dot_general(
            comp[:, i * LANES : (i + 1) * LANES],
            comp[:, i * LANES :],
            (((0,), (0,)), ((), ())),
            preferred_element_type=F32,
        )
        row_part = row_part / total_rows
        for j in range(i, n_blocks):
            number = blocks.index((i, j))
            for t in range(per_block):
                piece, slot = divmod(number * per_block + t, per_piece)
                gram_send[piece, slot] = row_part[
                    t * TILE : (t + 1) * TILE, (j - i) * LANES : (j - i + 1) * LANES
                ].astype(BF16)
    for t in range(len(blocks) * per_block, n_entity * per_piece):
        piece, slot = divmod(t, per_piece)
        gram_send[piece, slot] = jnp.zeros((TILE, LANES), BF16)

    pl.semaphore_wait(barrier, n_entity - 1)
    send_all(
        n_entity,
        lambda hop, peer: pltpu.make_async_remote_copy(
            src_ref=gram_send.at[peer],
            dst_ref=gram_recv.at[hop - 1],
            send_sem=send_sem.at[0],
            recv_sem=recv_sem.at[0],
            device_id={"entity": peer},
            device_id_type=MESH,
        ),
    )
    send_all(
        n_entity,
        lambda hop, peer: pltpu.make_async_remote_copy(
            src_ref=query_all.at[me],
            dst_ref=query_all.at[me],
            send_sem=send_sem.at[1],
            recv_sem=recv_sem.at[1],
            device_id={"entity": peer},
            device_id_type=MESH,
        ),
    )
    wait_bytes(gram_recv, recv_sem.at[0])
    total = gram_send[me].astype(F32)
    for k in range(n_entity - 1):
        total = total + gram_recv[k].astype(F32)
    gram_all[me] = total.astype(gram_all.dtype)
    send_all(
        n_entity,
        lambda hop, peer: pltpu.make_async_remote_copy(
            src_ref=gram_all.at[me],
            dst_ref=gram_all.at[me],
            send_sem=send_sem.at[2],
            recv_sem=recv_sem.at[2],
            device_id={"entity": peer},
            device_id_type=MESH,
        ),
    )
    wait_bytes(query_all.at[pl.ds(0, n_entity - 1)], recv_sem.at[1])
    for k in range(n_entity):
        query_f32[k * count : (k + 1) * count, :] = query_all[k].astype(F32)

    wait_bytes(gram_all.at[pl.ds(0, n_entity - 1)], recv_sem.at[2])
    for number, (i, j) in enumerate(blocks):
        for t in range(per_block):
            piece, slot = divmod(number * per_block + t, per_piece)
            gram[
                i * LANES + t * TILE : i * LANES + (t + 1) * TILE, j * LANES : (j + 1) * LANES
            ] = gram_all[piece, slot].astype(F32)
        if i != j:
            gram[j * LANES : (j + 1) * LANES, i * LANES : (i + 1) * LANES] = gram[
                i * LANES : (i + 1) * LANES, j * LANES : (j + 1) * LANES
            ].T

    row_ids = lax.broadcasted_iota(jnp.int32, (width, width), 0)
    col_ids = lax.broadcasted_iota(jnp.int32, (width, width), 1)
    identity = (row_ids == col_ids).astype(F32)
    full = gram[...] + RIDGE * identity
    squares = jnp.sum(full * full, axis=1, keepdims=True)
    frob_norm = jnp.sqrt(jnp.sum(squares, axis=0, keepdims=True) + EPSILON)
    first = full / frob_norm
    first_pair = split(first)
    second = product(first_pair, first_pair)
    inner = split(second - 4.5 * first)
    z_two = (36.0 * identity - 39.0 * first + 6.75 * second + product(inner, inner)) * (1.0 / 16.0)
    z_pair = split(z_two)
    y_pair = split(product(first_pair, z_pair))
    q_pair = split(product(z_pair, z_pair))
    z_three = 1.5 * z_two - 0.5 * product(y_pair, q_pair)
    whitener = (z_three / jnp.sqrt(frob_norm)).astype(BF16)

    white_slab = dot(comp[...], whitener).astype(BF16)
    white_query = dot(query_f32[...].astype(BF16), whitener).astype(BF16)
    scores = lax.dot_general(
        white_query, white_slab, (((1,), (1,)), ((), ())), preferred_element_type=F32
    ) * width ** (-0.5)
    top = jnp.max(scores, axis=1, keepdims=True)
    weights = jnp.exp(scores - top)
    denom = jnp.sum(weights, axis=1, keepdims=True)
    lane = lax.broadcasted_iota(jnp.int32, stats.shape, 1)
    stats[...] = jnp.where(lane == 0, top, denom)
    send_all(
        n_entity,
        lambda hop, peer: pltpu.make_async_remote_copy(
            src_ref=stats.at[pl.ds(pl.multiple_of(peer * count, count), count)],
            dst_ref=stats_recv.at[hop - 1],
            send_sem=send_sem.at[3],
            recv_sem=recv_sem.at[3],
            device_id={"entity": peer},
            device_id_type=MESH,
        ),
    )
    sums[...] = dot(weights.astype(BF16), white_slab)
    for k in range(n_entity):
        sums_send[k] = sums[k * count : (k + 1) * count, :].astype(sums_send.dtype)
    send_all(
        n_entity,
        lambda hop, peer: pltpu.make_async_remote_copy(
            src_ref=sums_send.at[peer],
            dst_ref=sums_recv.at[hop - 1],
            send_sem=send_sem.at[4],
            recv_sem=recv_sem.at[4],
            device_id={"entity": peer},
            device_id_type=MESH,
        ),
    )
    own = pl.ds(pl.multiple_of(me * count, count), count)
    own_stats = stats[own, :]
    own_sums = sums[own, :]
    wait_bytes(stats_recv, recv_sem.at[3])
    tops = [own_stats[:, 0:1]] + [stats_recv[k][:, 0:1] for k in range(n_entity - 1)]
    denoms = [own_stats[:, 1:2]] + [stats_recv[k][:, 1:2] for k in range(n_entity - 1)]
    row_top = functools.reduce(jnp.maximum, tops)
    factors = [jnp.exp(t - row_top) for t in tops]
    denom_all = functools.reduce(jnp.add, [f * d for f, d in zip(factors, denoms)])
    shares = [f / denom_all for f in factors]
    wait_bytes(sums_recv, recv_sem.at[4])
    result = own_sums * shares[0]
    for k in range(n_entity - 1):
        result = result + sums_recv[k].astype(F32) * shares[k + 1]
    out_ref[...] = result

    wait_bytes(gram_recv, send_sem.at[0])
    wait_bytes(query_all.at[pl.ds(0, n_entity - 1)], send_sem.at[1])
    wait_bytes(gram_all.at[pl.ds(0, n_entity - 1)], send_sem.at[2])
    wait_bytes(stats_recv, send_sem.at[3])
    wait_bytes(sums_recv, send_sem.at[4])


def solution(mesh):
    n_entity = mesh.shape["entity"]

    def per_device(companies, queries):
        rows, width = companies.shape
        count = queries.shape[0]
        n_blocks = width // LANES
        tiles = n_blocks * (n_blocks + 1) // 2 * (LANES // TILE)
        per_piece = -(-tiles // n_entity)
        return pl.pallas_call(
            functools.partial(kernel, n_entity),
            out_shape=jax.ShapeDtypeStruct((count, width), F32),
            in_specs=[
                pl.BlockSpec(memory_space=pl.ANY),
                pl.BlockSpec(memory_space=pltpu.VMEM),
            ],
            out_specs=pl.BlockSpec(memory_space=pltpu.VMEM),
            scratch_shapes=[
                pltpu.VMEM((rows, width), BF16),
                pltpu.VMEM((n_entity, count, width), BF16),
                pltpu.VMEM((n_entity * count, width), F32),
                pltpu.VMEM((n_entity, per_piece, TILE, LANES), BF16),
                pltpu.VMEM((n_entity - 1, per_piece, TILE, LANES), BF16),
                pltpu.VMEM((n_entity, per_piece, TILE, LANES), BF16),
                pltpu.VMEM((width, width), F32),
                pltpu.VMEM((n_entity * count, width), F32),
                pltpu.VMEM((n_entity, count, width), BF16),
                pltpu.VMEM((n_entity - 1, count, width), BF16),
                pltpu.VMEM((n_entity * count, LANES), F32),
                pltpu.VMEM((n_entity - 1, count, LANES), F32),
                pltpu.SemaphoreType.DMA,
                pltpu.SemaphoreType.DMA((5,)),
                pltpu.SemaphoreType.DMA((5,)),
            ],
            compiler_params=pltpu.CompilerParams(
                collective_id=0, has_side_effects=True, vmem_limit_bytes=48 << 20
            ),
            name="whiten_pool",
        )(companies, queries)

    return jax.shard_map(
        per_device,
        mesh=mesh,
        in_specs=(P("entity", None), P(("news", "entity"), None)),
        out_specs=P(("news", "entity"), None),
        check_vma=False,
    )
```

```python
import functools

import jax
import jax.numpy as jnp
from jax import lax
from jax.experimental import pallas as pl
from jax.experimental.pallas import tpu as pltpu
from jax.sharding import PartitionSpec as P

RIDGE = 0.05
EPSILON = 1e-06
MESH = pl.DeviceIdType.MESH
LANES = 128
TILE = 16
F32 = jnp.float32
BF16 = jnp.bfloat16


def dot(first_mat, second_mat):
    return jnp.dot(first_mat, second_mat, preferred_element_type=F32)


def product(first_mat, second_mat):
    return dot(first_mat.astype(BF16), second_mat.astype(BF16))


def remote(src_ref, dst_ref, sems, number, peer):
    send_sem, recv_sem = sems
    return pltpu.make_async_remote_copy(
        src_ref=src_ref,
        dst_ref=dst_ref,
        send_sem=send_sem.at[number],
        recv_sem=recv_sem.at[number],
        device_id={"entity": peer},
        device_id_type=MESH,
    )


def wait_bytes(ref, sem):
    pltpu.make_async_copy(ref, ref, sem).wait()


def kernel(
    n_entity,
    comp_hbm,
    query_hbm,
    out_ref,
    comp,
    query_all,
    query_f32,
    gram_send,
    gram_pair,
    gram_recv,
    gram_all,
    gram,
    sums,
    sums_send,
    sums_recv,
    stats,
    stats_recv,
    load_sem,
    send_sem,
    recv_sem,
):
    rows, width = comp.shape
    count = query_hbm.shape[0]
    total_rows = rows * n_entity
    n_blocks = width // LANES
    per_piece = gram_send.shape[1]
    me = lax.axis_index("entity")
    half = n_entity // 2
    chip, core = me // 2, lax.rem(me, 2)
    sibling = me + 1 - 2 * core
    my_slot = core * half + chip
    sems = (send_sem, recv_sem)

    load = pltpu.make_async_copy(comp_hbm, comp, load_sem.at[0])
    load.start()
    load_query = pltpu.make_async_copy(query_hbm, query_all.at[my_slot], load_sem.at[1])
    load_query.start()
    barrier = pltpu.get_barrier_semaphore()
    for hop in range(1, n_entity):
        pl.semaphore_signal(
            barrier,
            inc=1,
            device_id={"entity": lax.rem(me + hop, n_entity)},
            device_id_type=MESH,
        )
    load.wait()

    blocks = [(i, j) for i in range(n_blocks) for j in range(i, n_blocks)]
    per_block = LANES // TILE
    partial = {}
    for i in range(n_blocks):
        row_part = lax.dot_general(
            comp[:, i * LANES : (i + 1) * LANES],
            comp[:, i * LANES :],
            (((0,), (0,)), ((), ())),
            preferred_element_type=F32,
        )
        row_part = row_part / total_rows
        for j in range(i, n_blocks):
            number = blocks.index((i, j))
            for t in range(per_block):
                piece, slot = divmod(number * per_block + t, per_piece)
                gram_send[piece, slot] = row_part[
                    t * TILE : (t + 1) * TILE, (j - i) * LANES : (j - i + 1) * LANES
                ].astype(BF16)
    for t in range(len(blocks) * per_block, n_entity * per_piece):
        piece, slot = divmod(t, per_piece)
        gram_send[piece, slot] = jnp.zeros((TILE, LANES), BF16)

    load_query.wait()
    pl.semaphore_wait(barrier, n_entity - 1)

    own_half = pl.ds(core * half, half)
    other_half = pl.ds((1 - core) * half, half)
    peers = [(hop, lax.rem(chip + hop, half)) for hop in range(1, half)]
    to_pair = remote(gram_send.at[other_half], gram_pair, sems, 0, sibling)
    to_pair.start()
    to_pair.wait_recv()
    for k in range(half):
        gram_pair[k] = (gram_pair[k].astype(F32) + gram_send[core * half + k].astype(F32)).astype(
            gram_pair.dtype
        )
    for hop, there in peers:
        remote(gram_pair.at[there], gram_recv.at[hop - 1], sems, 1, 2 * there + core).start()
    total = gram_pair[chip].astype(F32)
    wait_bytes(gram_recv, recv_sem.at[1])
    for hop, there in peers:
        remote(query_all.at[my_slot], query_all.at[my_slot], sems, 2, 2 * there + core).start()
    for k in range(half - 1):
        total = total + gram_recv[k].astype(F32)
    gram_all[my_slot] = total.astype(gram_all.dtype)
    for hop, there in peers:
        remote(gram_all.at[my_slot], gram_all.at[my_slot], sems, 3, 2 * there + core).start()
    wait_bytes(gram_all.at[pl.ds(0, half - 1)], recv_sem.at[3])
    gram_forward = remote(gram_all.at[own_half], gram_all.at[own_half], sems, 4, sibling)
    gram_forward.start()
    wait_bytes(query_all.at[pl.ds(0, half - 1)], recv_sem.at[2])
    query_forward = remote(query_all.at[own_half], query_all.at[own_half], sems, 5, sibling)
    query_forward.start()

    def unpack(first_tile, last_tile):
        for number, (i, j) in enumerate(blocks):
            for t in range(per_block):
                tile = number * per_block + t
                if first_tile <= tile < last_tile:
                    piece, slot = divmod(tile, per_piece)
                    gram[
                        i * LANES + t * TILE : i * LANES + (t + 1) * TILE,
                        j * LANES : (j + 1) * LANES,
                    ] = gram_all[piece, slot].astype(F32)

    middle, last = half * per_piece, n_entity * per_piece
    pl.when(core == 0)(lambda: unpack(0, middle))
    pl.when(core == 1)(lambda: unpack(middle, last))
    gram_forward.wait_recv()
    pl.when(core == 0)(lambda: unpack(middle, last))
    pl.when(core == 1)(lambda: unpack(0, middle))
    for i, j in blocks:
        if i != j:
            gram[j * LANES : (j + 1) * LANES, i * LANES : (i + 1) * LANES] = gram[
                i * LANES : (i + 1) * LANES, j * LANES : (j + 1) * LANES
            ].T

    row_ids = lax.broadcasted_iota(jnp.int32, (width, width), 0)
    col_ids = lax.broadcasted_iota(jnp.int32, (width, width), 1)
    identity = (row_ids == col_ids).astype(F32)
    full = gram[...] + RIDGE * identity
    squares = jnp.sum(full * full, axis=1, keepdims=True)
    frob_norm = jnp.sqrt(jnp.sum(squares, axis=0, keepdims=True) + EPSILON)
    first = full * (1.0 / frob_norm)
    second = product(first, first)
    inner = second - 4.5 * first
    z_rest = (6.75 * second - 39.0 * first + product(inner, inner)) * (1.0 / 16.0)
    y_two = 2.25 * first + product(first, z_rest)
    q_rest = 4.5 * z_rest + product(z_rest, z_rest)
    z_three = (
        3.375 * identity + 1.5 * z_rest - 2.53125 * y_two - 0.5 * product(y_two, q_rest)
    )
    whitener = (z_three * (1.0 / jnp.sqrt(frob_norm))).astype(BF16)

    white_slab = dot(comp[...], whitener).astype(BF16)
    query_forward.wait_recv()
    for k in range(n_entity):
        query_f32[k * count : (k + 1) * count, :] = query_all[k].astype(F32)
    white_query = dot(query_f32[...].astype(BF16), whitener).astype(BF16)
    scores = lax.dot_general(
        white_query, white_slab, (((1,), (1,)), ((), ())), preferred_element_type=F32
    ) * width ** (-0.5)
    top = jnp.max(scores, axis=1, keepdims=True)
    weights = jnp.exp(scores - top)
    denom = jnp.sum(weights, axis=1, keepdims=True)
    lane = lax.broadcasted_iota(jnp.int32, stats.shape, 1)
    stats[...] = jnp.where(lane == 0, top, denom)
    others = [(hop, lax.rem(me + hop, n_entity)) for hop in range(1, n_entity)]
    slots = [lax.rem(peer, 2) * half + peer // 2 for _, peer in others]
    for (hop, peer), there in zip(others, slots):
        remote(
            stats.at[pl.ds(pl.multiple_of(there * count, count), count)],
            stats_recv.at[hop - 1],
            sems,
            6,
            peer,
        ).start()
    sums[...] = dot(weights.astype(BF16), white_slab)
    for k in range(n_entity):
        sums_send[k] = sums[k * count : (k + 1) * count, :].astype(sums_send.dtype)
    for (hop, peer), there in zip(others, slots):
        remote(sums_send.at[there], sums_recv.at[hop - 1], sems, 7, peer).start()
    own = pl.ds(pl.multiple_of(my_slot * count, count), count)
    own_stats = stats[own, :]
    own_sums = sums[own, :]
    wait_bytes(stats_recv, recv_sem.at[6])
    tops = [own_stats[:, 0:1]] + [stats_recv[k][:, 0:1] for k in range(n_entity - 1)]
    denoms = [own_stats[:, 1:2]] + [stats_recv[k][:, 1:2] for k in range(n_entity - 1)]
    row_top = functools.reduce(jnp.maximum, tops)
    factors = [jnp.exp(t - row_top) for t in tops]
    denom_all = functools.reduce(jnp.add, [f * d for f, d in zip(factors, denoms)])
    shares = [f / denom_all for f in factors]
    wait_bytes(sums_recv, recv_sem.at[7])
    result = own_sums * shares[0]
    for k in range(n_entity - 1):
        result = result + sums_recv[k].astype(F32) * shares[k + 1]
    out_ref[...] = result

    to_pair.wait_send()
    wait_bytes(gram_recv, send_sem.at[1])
    wait_bytes(query_all.at[pl.ds(0, half - 1)], send_sem.at[2])
    wait_bytes(gram_all.at[pl.ds(0, half - 1)], send_sem.at[3])
    gram_forward.wait_send()
    query_forward.wait_send()
    wait_bytes(stats_recv, send_sem.at[6])
    wait_bytes(sums_recv, send_sem.at[7])


def solution(mesh):
    n_entity = mesh.shape["entity"]

    def per_device(companies, queries):
        rows, width = companies.shape
        count = queries.shape[0]
        n_blocks = width // LANES
        tiles = n_blocks * (n_blocks + 1) // 2 * (LANES // TILE)
        per_piece = -(-tiles // n_entity)
        return pl.pallas_call(
            functools.partial(kernel, n_entity),
            out_shape=jax.ShapeDtypeStruct((count, width), F32),
            in_specs=[
                pl.BlockSpec(memory_space=pltpu.HBM),
                pl.BlockSpec(memory_space=pltpu.HBM),
            ],
            out_specs=pl.BlockSpec(memory_space=pltpu.VMEM),
            scratch_shapes=[
                pltpu.VMEM((rows, width), BF16),
                pltpu.VMEM((n_entity, count, width), BF16),
                pltpu.VMEM((n_entity * count, width), F32),
                pltpu.VMEM((n_entity, per_piece, TILE, LANES), BF16),
                pltpu.VMEM((n_entity // 2, per_piece, TILE, LANES), BF16),
                pltpu.VMEM((n_entity // 2 - 1, per_piece, TILE, LANES), BF16),
                pltpu.VMEM((n_entity, per_piece, TILE, LANES), BF16),
                pltpu.VMEM((width, width), F32),
                pltpu.VMEM((n_entity * count, width), F32),
                pltpu.VMEM((n_entity, count, width), BF16),
                pltpu.VMEM((n_entity - 1, count, width), BF16),
                pltpu.VMEM((n_entity * count, LANES), F32),
                pltpu.VMEM((n_entity - 1, count, LANES), F32),
                pltpu.SemaphoreType.DMA((2,)),
                pltpu.SemaphoreType.DMA((8,)),
                pltpu.SemaphoreType.DMA((8,)),
            ],
            compiler_params=pltpu.CompilerParams(
                collective_id=0, has_side_effects=True, vmem_limit_bytes=48 << 20
            ),
            name="whiten_pool",
        )(companies, queries)

    return jax.shard_map(
        per_device,
        mesh=mesh,
        in_specs=(P("entity", None), P(("news", "entity"), None)),
        out_specs=P(("news", "entity"), None),
        check_vma=False,
    )
```

```python
import functools

import jax
import jax.numpy as jnp
from jax import lax
from jax.experimental import pallas as pl
from jax.experimental.pallas import tpu as pltpu
from jax.sharding import PartitionSpec as P

RIDGE = 0.05
EPSILON = 1e-06
MESH = pl.DeviceIdType.MESH
LANES = 128
TILE = 16
F32 = jnp.float32
BF16 = jnp.bfloat16


def dot(first_mat, second_mat):
    return jnp.dot(first_mat, second_mat, preferred_element_type=F32)


def product(first_mat, second_mat):
    return dot(first_mat.astype(BF16), second_mat.astype(BF16))


def three_parts(value):
    high = value.astype(BF16).astype(F32)
    middle = (value - high).astype(BF16).astype(F32)
    return [high, middle, value - high - middle]


def remote(src_ref, dst_ref, sems, number, peer):
    send_sem, recv_sem = sems
    return pltpu.make_async_remote_copy(
        src_ref=src_ref,
        dst_ref=dst_ref,
        send_sem=send_sem.at[number],
        recv_sem=recv_sem.at[number],
        device_id={"entity": peer},
        device_id_type=MESH,
    )


def wait_bytes(ref, sem):
    pltpu.make_async_copy(ref, ref, sem).wait()


def kernel(
    n_entity,
    comp_hbm,
    query_hbm,
    out_ref,
    comp,
    query_all,
    query_f32,
    gram_send,
    gram_pair,
    gram_recv,
    gram_all,
    gram,
    sums,
    sums_pair,
    stats,
    stats_pair,
    part_send,
    part_recv,
    load_sem,
    send_sem,
    recv_sem,
):
    rows, width = comp.shape
    count = query_hbm.shape[0]
    total_rows = rows * n_entity
    n_blocks = width // LANES
    per_piece = gram_send.shape[1]
    me = lax.axis_index("entity")
    half = n_entity // 2
    chip, core = me // 2, lax.rem(me, 2)
    sibling = me + 1 - 2 * core
    my_slot = core * half + chip
    sems = (send_sem, recv_sem)

    load = pltpu.make_async_copy(comp_hbm, comp, load_sem.at[0])
    load.start()
    load_query = pltpu.make_async_copy(query_hbm, query_all.at[my_slot], load_sem.at[1])
    load_query.start()
    barrier = pltpu.get_barrier_semaphore()
    peers = [(hop, lax.rem(chip + hop, half)) for hop in range(1, half)]
    for partner in [sibling] + [2 * there + core for _, there in peers]:
        pl.semaphore_signal(
            barrier, inc=1, device_id={"entity": partner}, device_id_type=MESH
        )
    load.wait()

    blocks = [(i, j) for i in range(n_blocks) for j in range(i, n_blocks)]
    per_block = LANES // TILE
    partial = {}
    for i in range(n_blocks):
        row_part = lax.dot_general(
            comp[:, i * LANES : (i + 1) * LANES],
            comp[:, i * LANES :],
            (((0,), (0,)), ((), ())),
            preferred_element_type=F32,
        )
        row_part = row_part / total_rows
        for j in range(i, n_blocks):
            number = blocks.index((i, j))
            for t in range(per_block):
                piece, slot = divmod(number * per_block + t, per_piece)
                gram_send[piece, slot] = row_part[
                    t * TILE : (t + 1) * TILE, (j - i) * LANES : (j - i + 1) * LANES
                ].astype(BF16)
    for t in range(len(blocks) * per_block, n_entity * per_piece):
        piece, slot = divmod(t, per_piece)
        gram_send[piece, slot] = jnp.zeros((TILE, LANES), BF16)

    load_query.wait()
    pl.semaphore_wait(barrier, half)

    own_half = pl.ds(core * half, half)
    other_half = pl.ds((1 - core) * half, half)
    to_pair = remote(gram_send.at[other_half], gram_pair, sems, 0, sibling)
    to_pair.start()
    for hop, there in peers:
        remote(query_all.at[my_slot], query_all.at[my_slot], sems, 2, 2 * there + core).start()
    to_pair.wait_recv()
    for k in range(half):
        gram_pair[k] = (gram_pair[k].astype(F32) + gram_send[core * half + k].astype(F32)).astype(
            gram_pair.dtype
        )
    for hop, there in peers:
        remote(gram_pair.at[there], gram_recv.at[hop - 1], sems, 1, 2 * there + core).start()
    total = gram_pair[chip].astype(F32)
    wait_bytes(gram_recv, recv_sem.at[1])
    for k in range(half - 1):
        total = total + gram_recv[k].astype(F32)
    gram_all[my_slot] = total.astype(gram_all.dtype)
    for hop, there in peers:
        remote(gram_all.at[my_slot], gram_all.at[my_slot], sems, 3, 2 * there + core).start()
    wait_bytes(query_all.at[pl.ds(0, half - 1)], recv_sem.at[2])
    query_forward = remote(query_all.at[own_half], query_all.at[own_half], sems, 5, sibling)
    query_forward.start()
    wait_bytes(gram_all.at[pl.ds(0, half - 1)], recv_sem.at[3])
    gram_forward = remote(gram_all.at[own_half], gram_all.at[own_half], sems, 4, sibling)
    gram_forward.start()

    def unpack(first_tile, last_tile):
        for number, (i, j) in enumerate(blocks):
            for t in range(per_block):
                tile = number * per_block + t
                if first_tile <= tile < last_tile:
                    piece, slot = divmod(tile, per_piece)
                    gram[
                        i * LANES + t * TILE : i * LANES + (t + 1) * TILE,
                        j * LANES : (j + 1) * LANES,
                    ] = gram_all[piece, slot].astype(F32)

    middle, last = half * per_piece, n_entity * per_piece
    pl.when(core == 0)(lambda: unpack(0, middle))
    pl.when(core == 1)(lambda: unpack(middle, last))
    gram_forward.wait_recv()
    pl.when(core == 0)(lambda: unpack(middle, last))
    pl.when(core == 1)(lambda: unpack(0, middle))
    for i, j in blocks:
        if i != j:
            gram[j * LANES : (j + 1) * LANES, i * LANES : (i + 1) * LANES] = gram[
                i * LANES : (i + 1) * LANES, j * LANES : (j + 1) * LANES
            ].T

    row_ids = lax.broadcasted_iota(jnp.int32, (width, width), 0)
    col_ids = lax.broadcasted_iota(jnp.int32, (width, width), 1)
    identity = (row_ids == col_ids).astype(F32)
    full = gram[...] + RIDGE * identity
    squares = jnp.sum(full * full, axis=1, keepdims=True)
    frob_norm = jnp.sqrt(jnp.sum(squares, axis=0, keepdims=True) + EPSILON)
    first = full * (1.0 / frob_norm)
    second = product(first, first)
    inner = second - 4.5 * first
    z_rest = (6.75 * second - 39.0 * first + product(inner, inner)) * (1.0 / 16.0)
    y_two = 2.25 * first + product(first, z_rest)
    q_rest = 4.5 * z_rest + product(z_rest, z_rest)
    z_three = (
        3.375 * identity + 1.5 * z_rest - 2.53125 * y_two - 0.5 * product(y_two, q_rest)
    )
    whitener = (z_three * (1.0 / jnp.sqrt(frob_norm))).astype(BF16)

    white_slab = dot(comp[...], whitener).astype(BF16)
    query_forward.wait_recv()
    for k in range(n_entity):
        query_f32[k * count : (k + 1) * count, :] = query_all[k].astype(F32)
    white_query = dot(query_f32[...].astype(BF16), whitener).astype(BF16)
    scores = lax.dot_general(
        white_query, white_slab, (((1,), (1,)), ((), ())), preferred_element_type=F32
    ) * width ** (-0.5)
    top = jnp.max(scores, axis=1, keepdims=True)
    weights = jnp.exp(scores - top)
    denom = jnp.sum(weights, axis=1, keepdims=True)
    lane = lax.broadcasted_iota(jnp.int32, stats.shape, 1)
    stats[...] = jnp.where(lane == 0, top, denom)
    own_rows = pl.ds(pl.multiple_of(core * half * count, half * count), half * count)
    other_rows = pl.ds(pl.multiple_of((1 - core) * half * count, half * count), half * count)
    stats_to_pair = remote(stats.at[other_rows], stats_pair, sems, 6, sibling)
    stats_to_pair.start()
    sums[...] = dot(weights.astype(BF16), white_slab)
    sums_to_pair = remote(sums.at[other_rows], sums_pair, sems, 7, sibling)
    sums_to_pair.start()
    own_stats = stats[own_rows, :]
    stats_to_pair.wait_recv()
    pair_top = jnp.maximum(own_stats[:, 0:1], stats_pair[:, 0:1])
    own_factor = jnp.exp(own_stats[:, 0:1] - pair_top)
    pair_factor = jnp.exp(stats_pair[:, 0:1] - pair_top)
    pair_denom = own_factor * own_stats[:, 1:2] + pair_factor * stats_pair[:, 1:2]
    tail_lane = lax.broadcasted_iota(jnp.int32, stats_pair.shape, 1)
    tail = jnp.zeros(stats_pair.shape, F32)
    for number, part in enumerate(three_parts(pair_top) + three_parts(pair_denom)):
        tail = jnp.where(tail_lane == number, part, tail)
    sums_to_pair.wait_recv()
    merged = own_factor * sums[own_rows, :] + pair_factor * sums_pair[...]
    for k in range(half):
        part_send[k, :, :width] = merged[k * count : (k + 1) * count, :].astype(BF16)
        part_send[k, :, width:] = tail[k * count : (k + 1) * count, :].astype(BF16)
    for hop, there in peers:
        remote(part_send.at[there], part_recv.at[hop - 1], sems, 8, 2 * there + core).start()
    wait_bytes(part_recv, recv_sem.at[8])
    parts = [part_send[chip]] + [part_recv[k] for k in range(half - 1)]
    tails = [part[:, width:].astype(F32) for part in parts]
    tops = [t[:, 0:1] + t[:, 1:2] + t[:, 2:3] for t in tails]
    denoms = [t[:, 3:4] + t[:, 4:5] + t[:, 5:6] for t in tails]
    row_top = functools.reduce(jnp.maximum, tops)
    factors = [jnp.exp(t - row_top) for t in tops]
    denom_all = functools.reduce(jnp.add, [f * d for f, d in zip(factors, denoms)])
    result = functools.reduce(
        jnp.add, [f * part[:, :width].astype(F32) for f, part in zip(factors, parts)]
    )
    out_ref[...] = result / denom_all

    to_pair.wait_send()
    wait_bytes(gram_recv, send_sem.at[1])
    wait_bytes(query_all.at[pl.ds(0, half - 1)], send_sem.at[2])
    wait_bytes(gram_all.at[pl.ds(0, half - 1)], send_sem.at[3])
    gram_forward.wait_send()
    query_forward.wait_send()
    stats_to_pair.wait_send()
    sums_to_pair.wait_send()
    wait_bytes(part_recv, send_sem.at[8])


def solution(mesh):
    n_entity = mesh.shape["entity"]

    def per_device(companies, queries):
        rows, width = companies.shape
        count = queries.shape[0]
        n_blocks = width // LANES
        tiles = n_blocks * (n_blocks + 1) // 2 * (LANES // TILE)
        per_piece = -(-tiles // n_entity)
        return pl.pallas_call(
            functools.partial(kernel, n_entity),
            out_shape=jax.ShapeDtypeStruct((count, width), F32),
            in_specs=[
                pl.BlockSpec(memory_space=pltpu.HBM),
                pl.BlockSpec(memory_space=pltpu.HBM),
            ],
            out_specs=pl.BlockSpec(memory_space=pltpu.VMEM),
            scratch_shapes=[
                pltpu.VMEM((rows, width), BF16),
                pltpu.VMEM((n_entity, count, width), BF16),
                pltpu.VMEM((n_entity * count, width), F32),
                pltpu.VMEM((n_entity, per_piece, TILE, LANES), BF16),
                pltpu.VMEM((n_entity // 2, per_piece, TILE, LANES), BF16),
                pltpu.VMEM((n_entity // 2 - 1, per_piece, TILE, LANES), BF16),
                pltpu.VMEM((n_entity, per_piece, TILE, LANES), BF16),
                pltpu.VMEM((width, width), F32),
                pltpu.VMEM((n_entity * count, width), F32),
                pltpu.VMEM((n_entity // 2 * count, width), F32),
                pltpu.VMEM((n_entity * count, LANES), F32),
                pltpu.VMEM((n_entity // 2 * count, LANES), F32),
                pltpu.VMEM((n_entity // 2, count, width + LANES), BF16),
                pltpu.VMEM((n_entity // 2 - 1, count, width + LANES), BF16),
                pltpu.SemaphoreType.DMA((2,)),
                pltpu.SemaphoreType.DMA((9,)),
                pltpu.SemaphoreType.DMA((9,)),
            ],
            compiler_params=pltpu.CompilerParams(
                collective_id=0, has_side_effects=True, vmem_limit_bytes=48 << 20
            ),
            name="whiten_pool",
        )(companies, queries)

    return jax.shard_map(
        per_device,
        mesh=mesh,
        in_specs=(P("entity", None), P(("news", "entity"), None)),
        out_specs=P(("news", "entity"), None),
        check_vma=False,
    )
```

```python
import functools

import jax
import jax.numpy as jnp
from jax import lax
from jax.experimental import pallas as pl
from jax.experimental.pallas import tpu as pltpu
from jax.sharding import PartitionSpec as P

RIDGE = 0.05
EPSILON = 1e-06
MESH = pl.DeviceIdType.MESH
LANES = 128
TILE = 16
F32 = jnp.float32
BF16 = jnp.bfloat16


def dot(first_mat, second_mat):
    return jnp.dot(first_mat, second_mat, preferred_element_type=F32)


def product(first_mat, second_mat):
    return dot(first_mat.astype(BF16), second_mat.astype(BF16))


def three_parts(value):
    high = value.astype(BF16).astype(F32)
    middle = (value - high).astype(BF16).astype(F32)
    return [high, middle, value - high - middle]


def remote(src_ref, dst_ref, sems, number, peer):
    send_sem, recv_sem = sems
    return pltpu.make_async_remote_copy(
        src_ref=src_ref,
        dst_ref=dst_ref,
        send_sem=send_sem.at[number],
        recv_sem=recv_sem.at[number],
        device_id={"entity": peer},
        device_id_type=MESH,
    )


def wait_bytes(ref, sem):
    pltpu.make_async_copy(ref, ref, sem).wait()


def kernel(
    n_entity,
    comp_hbm,
    query_hbm,
    out_ref,
    comp,
    query_all,
    query_f32,
    gram_send,
    gram_pair,
    gram_recv,
    gram_all,
    gram,
    part_send,
    part_recv,
    load_sem,
    send_sem,
    recv_sem,
):
    rows, width = comp.shape
    count = query_hbm.shape[0]
    total_rows = rows * n_entity
    n_blocks = width // LANES
    per_piece = gram_send.shape[1]
    me = lax.axis_index("entity")
    half = n_entity // 2
    chip, core = me // 2, lax.rem(me, 2)
    sibling = me + 1 - 2 * core
    my_slot = core * half + chip
    sems = (send_sem, recv_sem)

    load = pltpu.make_async_copy(comp_hbm, comp, load_sem.at[0])
    load.start()
    load_query = pltpu.make_async_copy(query_hbm, query_all.at[my_slot], load_sem.at[1])
    load_query.start()
    barrier = pltpu.get_barrier_semaphore()
    peers = [(hop, lax.rem(chip + hop, half)) for hop in range(1, half)]
    others = [(hop, lax.rem(me + hop, n_entity)) for hop in range(1, n_entity)]
    for _, partner in others:
        pl.semaphore_signal(
            barrier, inc=1, device_id={"entity": partner}, device_id_type=MESH
        )
    load.wait()

    blocks = [(i, j) for i in range(n_blocks) for j in range(i, n_blocks)]
    per_block = LANES // TILE
    partial = {}
    for i in range(n_blocks):
        row_part = lax.dot_general(
            comp[:, i * LANES : (i + 1) * LANES],
            comp[:, i * LANES :],
            (((0,), (0,)), ((), ())),
            preferred_element_type=F32,
        )
        row_part = row_part / total_rows
        for j in range(i, n_blocks):
            number = blocks.index((i, j))
            for t in range(per_block):
                piece, slot = divmod(number * per_block + t, per_piece)
                gram_send[piece, slot] = row_part[
                    t * TILE : (t + 1) * TILE, (j - i) * LANES : (j - i + 1) * LANES
                ].astype(BF16)
    for t in range(len(blocks) * per_block, n_entity * per_piece):
        piece, slot = divmod(t, per_piece)
        gram_send[piece, slot] = jnp.zeros((TILE, LANES), BF16)

    load_query.wait()
    pl.semaphore_wait(barrier, n_entity - 1)

    own_half = pl.ds(core * half, half)
    other_half = pl.ds((1 - core) * half, half)
    to_pair = remote(gram_send.at[other_half], gram_pair, sems, 0, sibling)
    to_pair.start()
    for hop, there in peers:
        remote(query_all.at[my_slot], query_all.at[my_slot], sems, 2, 2 * there + core).start()
    to_pair.wait_recv()
    for k in range(half):
        gram_pair[k] = (gram_pair[k].astype(F32) + gram_send[core * half + k].astype(F32)).astype(
            gram_pair.dtype
        )
    for hop, there in peers:
        remote(gram_pair.at[there], gram_recv.at[hop - 1], sems, 1, 2 * there + core).start()
    total = gram_pair[chip].astype(F32)
    wait_bytes(gram_recv, recv_sem.at[1])
    for k in range(half - 1):
        total = total + gram_recv[k].astype(F32)
    gram_all[my_slot] = total.astype(gram_all.dtype)
    for hop, there in peers:
        remote(gram_all.at[my_slot], gram_all.at[my_slot], sems, 3, 2 * there + core).start()
    wait_bytes(query_all.at[pl.ds(0, half - 1)], recv_sem.at[2])
    query_forward = remote(query_all.at[own_half], query_all.at[own_half], sems, 5, sibling)
    query_forward.start()
    wait_bytes(gram_all.at[pl.ds(0, half - 1)], recv_sem.at[3])
    gram_forward = remote(gram_all.at[own_half], gram_all.at[own_half], sems, 4, sibling)
    gram_forward.start()

    def unpack(first_tile, last_tile):
        for number, (i, j) in enumerate(blocks):
            for t in range(per_block):
                tile = number * per_block + t
                if first_tile <= tile < last_tile:
                    piece, slot = divmod(tile, per_piece)
                    gram[
                        i * LANES + t * TILE : i * LANES + (t + 1) * TILE,
                        j * LANES : (j + 1) * LANES,
                    ] = gram_all[piece, slot].astype(F32)

    middle, last = half * per_piece, n_entity * per_piece
    pl.when(core == 0)(lambda: unpack(0, middle))
    pl.when(core == 1)(lambda: unpack(middle, last))
    gram_forward.wait_recv()
    pl.when(core == 0)(lambda: unpack(middle, last))
    pl.when(core == 1)(lambda: unpack(0, middle))
    for i, j in blocks:
        if i != j:
            gram[j * LANES : (j + 1) * LANES, i * LANES : (i + 1) * LANES] = gram[
                i * LANES : (i + 1) * LANES, j * LANES : (j + 1) * LANES
            ].T

    row_ids = lax.broadcasted_iota(jnp.int32, (width, width), 0)
    col_ids = lax.broadcasted_iota(jnp.int32, (width, width), 1)
    identity = (row_ids == col_ids).astype(F32)
    full = gram[...] + RIDGE * identity
    squares = jnp.sum(full * full, axis=1, keepdims=True)
    frob_norm = jnp.sqrt(jnp.sum(squares, axis=0, keepdims=True) + EPSILON)
    first = full * (1.0 / frob_norm)
    second = product(first, first)
    inner = second - 4.5 * first
    z_rest = (6.75 * second - 39.0 * first + product(inner, inner)) * (1.0 / 16.0)
    y_two = 2.25 * first + product(first, z_rest)
    q_rest = 4.5 * z_rest + product(z_rest, z_rest)
    z_three = (
        3.375 * identity + 1.5 * z_rest - 2.53125 * y_two - 0.5 * product(y_two, q_rest)
    )
    whitener = (z_three * (1.0 / jnp.sqrt(frob_norm))).astype(BF16)

    white_slab = dot(comp[...], whitener).astype(BF16)
    query_forward.wait_recv()
    for k in range(n_entity):
        query_f32[k * count : (k + 1) * count, :] = query_all[k].astype(F32)
    white_query = dot(query_f32[...].astype(BF16), whitener).astype(BF16)
    scores = lax.dot_general(
        white_query, white_slab, (((1,), (1,)), ((), ())), preferred_element_type=F32
    ) * width ** (-0.5)
    top = jnp.max(scores, axis=1, keepdims=True)
    weights = jnp.exp(scores - top)
    denom = jnp.sum(weights, axis=1, keepdims=True)
    lane = lax.broadcasted_iota(jnp.int32, (n_entity * count, LANES), 1)
    tail = jnp.zeros(lane.shape, F32)
    for number, part in enumerate(three_parts(top) + three_parts(denom)):
        tail = jnp.where(lane == number, part, tail)
    summed = dot(weights.astype(BF16), white_slab)
    for k in range(n_entity):
        part_send[k, :, :width] = summed[k * count : (k + 1) * count, :].astype(BF16)
        part_send[k, :, width:] = tail[k * count : (k + 1) * count, :].astype(BF16)
    for hop, peer in others:
        there = lax.rem(peer, 2) * half + peer // 2
        remote(part_send.at[there], part_recv.at[hop - 1], sems, 6, peer).start()
    wait_bytes(part_recv, recv_sem.at[6])
    parts = [part_send[my_slot]] + [part_recv[k] for k in range(n_entity - 1)]
    tails = [part[:, width:].astype(F32) for part in parts]
    tops = [t[:, 0:1] + t[:, 1:2] + t[:, 2:3] for t in tails]
    denoms = [t[:, 3:4] + t[:, 4:5] + t[:, 5:6] for t in tails]
    row_top = functools.reduce(jnp.maximum, tops)
    factors = [jnp.exp(t - row_top) for t in tops]
    denom_all = functools.reduce(jnp.add, [f * d for f, d in zip(factors, denoms)])
    result = functools.reduce(
        jnp.add, [f * part[:, :width].astype(F32) for f, part in zip(factors, parts)]
    )
    out_ref[...] = result / denom_all

    to_pair.wait_send()
    wait_bytes(gram_recv, send_sem.at[1])
    wait_bytes(query_all.at[pl.ds(0, half - 1)], send_sem.at[2])
    wait_bytes(gram_all.at[pl.ds(0, half - 1)], send_sem.at[3])
    gram_forward.wait_send()
    query_forward.wait_send()
    wait_bytes(part_recv, send_sem.at[6])


def solution(mesh):
    n_entity = mesh.shape["entity"]

    def per_device(companies, queries):
        rows, width = companies.shape
        count = queries.shape[0]
        n_blocks = width // LANES
        tiles = n_blocks * (n_blocks + 1) // 2 * (LANES // TILE)
        per_piece = -(-tiles // n_entity)
        return pl.pallas_call(
            functools.partial(kernel, n_entity),
            out_shape=jax.ShapeDtypeStruct((count, width), F32),
            in_specs=[
                pl.BlockSpec(memory_space=pltpu.HBM),
                pl.BlockSpec(memory_space=pltpu.HBM),
            ],
            out_specs=pl.BlockSpec(memory_space=pltpu.VMEM),
            scratch_shapes=[
                pltpu.VMEM((rows, width), BF16),
                pltpu.VMEM((n_entity, count, width), BF16),
                pltpu.VMEM((n_entity * count, width), F32),
                pltpu.VMEM((n_entity, per_piece, TILE, LANES), BF16),
                pltpu.VMEM((n_entity // 2, per_piece, TILE, LANES), BF16),
                pltpu.VMEM((n_entity // 2 - 1, per_piece, TILE, LANES), BF16),
                pltpu.VMEM((n_entity, per_piece, TILE, LANES), BF16),
                pltpu.VMEM((width, width), F32),
                pltpu.VMEM((n_entity, count, width + LANES), BF16),
                pltpu.VMEM((n_entity - 1, count, width + LANES), BF16),
                pltpu.SemaphoreType.DMA((2,)),
                pltpu.SemaphoreType.DMA((7,)),
                pltpu.SemaphoreType.DMA((7,)),
            ],
            compiler_params=pltpu.CompilerParams(
                collective_id=0, has_side_effects=True, vmem_limit_bytes=48 << 20
            ),
            name="whiten_pool",
        )(companies, queries)

    return jax.shard_map(
        per_device,
        mesh=mesh,
        in_specs=(P("entity", None), P(("news", "entity"), None)),
        out_specs=P(("news", "entity"), None),
        check_vma=False,
    )
```
